256 devices in a mesh: dp: 32 (over z, y), expert: 8 (over x, core).
Axes of the slice: x: 4, y: 4, z: 8, core: 2. Of those that a mesh axis runs over, the one named last changes fastest.
Arguments:
- frames: bfloat16 [32768, 1024], P(('dp', 'expert')), may hold values from -24 to 24
- expert_ids: int32 [32768, 2], P(('dp', 'expert')), may hold values from 0 to 7, all different within a row; in each aligned block of 128 rows (0 to 127, 128 to 255, ...) at most 64 rows name the same one
- gate_weights: float32 [32768, 2], P(('dp', 'expert')), may hold values from 0.2 to 1
- cotangent: bfloat16 [32768, 1024], P(('dp', 'expert')), may hold values from -24 to 24
- w_in: bfloat16 [8, 1024, 2048], P('expert'), may hold values from -0.1875 to 0.1875
- w_out: bfloat16 [8, 2048, 1024], P('expert'), may hold values from -0.125 to 0.125
Outputs:
- mixed: bfloat16 [32768, 1024], P(('dp', 'expert'))
- grad_frames: bfloat16 [32768, 1024], P(('dp', 'expert'))
- grad_w_in: float32 [8, 1024, 2048], P('expert', 'dp')
- grad_w_out: float32 [8, 2048, 1024], P('expert', 'dp')
The draws below stay inside these ranges and needn't reach their ends.
Inputs may be any that keep to these rules, and one draw needn't show every extreme that they name: `expert_ids`: the two experts of a frame differ. Among the 128 frames of one device (aligned blocks of rows), no expert is named by more than 64 of them, and in some block one expert is named by exactly 64.
All inputs are finite; a program needn't handle non-finite values.
Results may differ from the reference program's by a relative error of at most 0.015.
Values may be sent and summed in bfloat16 or wider, within the bound.
No kernel may reach another device: no remote copies, remote signals or barrier semaphores. Data moves between devices by JAX's collectives and lax.ppermute only.
A program may use at most 128 MiB of HBM per device.

```python
import math
import jax
import jax.numpy as jnp
import numpy as np
from jax import lax

D = 1024
HID = 2048
TOK_DEV = 128
EXPERTS = 8
CAP = 64
TOKENS = 32768
N_DP = 32
N_EXPERT = 8


def strengthened(values, own_key, source, target, parts, factor):
    def block_of(axis_at):
        return (jnp.arange(values.shape[axis_at]) // (values.shape[axis_at] // parts)).reshape((-1,) + (1,) * (values.ndim - 1 - axis_at))

    near = jax.random.permutation(own_key, parts)[block_of(target)]
    second = (block_of(target) + parts // 2) % parts
    return jnp.where((block_of(source) == near) | (block_of(source) == second), factor * values, values)


def shard_levels(stream_key, extent, cuts, least, largest):
    def one(position, shards_of):
        steps = jax.random.uniform(jax.random.fold_in(jax.random.fold_in(stream_key, 6), position), (shards_of,), jnp.float32, least / len(cuts), largest / len(cuts))
        return jnp.repeat(jnp.exp(steps), extent[position] // shards_of).reshape((-1,) + (1,) * (len(extent) - position - 1))

    level = one(*cuts[0])
    for cut in cuts[1:]:
        level = level * one(*cut)
    return level


def routed_block(own_key, own, number, rows, number_of, top, reach, lean):
    ranking = jax.random.permutation(own_key, number_of)
    crowded, usual = load_shares(number_of, rows * top, reach, lean, True), load_shares(number_of, rows * top, reach, lean, False)
    places = jnp.arange(number_of)

    def named(lengths, rotation):
        used = int((lengths > 0).sum())
        fixed = max(1, used // 4)
        shifted = fixed + (places - fixed + rotation * (used - fixed)) % max(1, number_of - fixed)
        return jnp.zeros((number_of,), jnp.int32).at[ranking[jnp.where(places < fixed, places, shifted)]].set(jnp.asarray(lengths, jnp.int32))

    lengths = jnp.where(number % 4 == 0, named(crowded, number // 4), named(usual, number - number // 4 - 1))
    mixed = jax.random.permutation(jax.random.fold_in(own, 3), number_of)
    giver, taker = mixed[0:number_of // 2 * 2:2], mixed[1:number_of // 2 * 2:2]
    slack = jnp.minimum(lengths[giver] - 1, reach - lengths[taker]) // 2
    slack = jnp.where((giver == ranking[0]) | (taker == ranking[0]) | (lengths[taker] == 0), 0, jnp.maximum(slack, 0))
    shifted = jax.random.randint(jax.random.fold_in(own, 4), (number_of // 2,), 0, 1 << 20) % (slack + 1)
    lengths = lengths.at[giver].add(-shifted).at[taker].add(shifted)
    items = jnp.searchsorted(jnp.cumsum(lengths), jnp.arange(rows * top), side="right").astype(jnp.int32)
    listing = items.reshape(top, rows).T
    listing = listing[jax.random.permutation(jax.random.fold_in(own, 1), rows)]
    rotation = jax.random.randint(jax.random.fold_in(own, 2), (rows, 1), 0, top)
    return jnp.take_along_axis(listing, (jnp.arange(top)[None, :] + rotation) % top, axis=1)


def load_shares(amount, total, bound, slope, full):
    portions = [(1 << 20) // math.isqrt(standing ** slope) + 1 for standing in range(1, amount + 1)]
    largest = bound if full else min(bound, max(-(-total // amount), total * portions[0] // sum(portions)))
    least = 1 if total - largest >= amount - 1 else 0
    counts, rest = [largest] + [least] * (amount - 1), total - largest - least * (amount - 1)
    while rest > 0:
        free = [i for i in range(1, amount) if counts[i] < largest] or [i for i in range(1, amount) if counts[i] < bound]
        pool, left = sum([portions[i] for i in free]), rest
        for i in free:
            addition = min(bound - counts[i], max(1, left * portions[i] // pool), rest)
            counts[i] = counts[i] + addition
            rest = rest - addition
    return np.array(counts)


def noise(stream_key, extent, deviation, limit, pieces=(), held_as=jnp.bfloat16):
    result = deviation * jax.random.normal(stream_key, extent, jnp.float32)
    if pieces:
        result = result * shard_levels(stream_key, extent, pieces, -0.22, 0.18)
    return jnp.clip(result, -limit, limit).astype(held_as)


def heavy_noise(key, extent, spread, bound, cuts, heavy, kind=jnp.bfloat16):
    entries = spread * jax.random.normal(key, extent, jnp.float32)
    if cuts:
        entries = entries * shard_levels(key, extent, cuts, -0.22, 0.18)
    return jnp.clip(strengthened(entries, jax.random.fold_in(key, 3), *heavy), -bound, bound).astype(kind)


def setup_inputs(seed: int = 0) -> dict:
    key_of = jax.random.split(jax.random.key(seed), 7)
    frames = heavy_noise(key_of[0], (TOKENS, D), 1.0, 24.0, ((0, 256),), (0, 1, 256, 6.0))
    expert_ids_keys = jax.random.split(jax.random.fold_in(key_of[1], 1), TOKENS // TOK_DEV)
    expert_ids_turns = jax.random.permutation(jax.random.fold_in(key_of[1], 3), TOKENS // TOK_DEV)
    expert_ids = jax.vmap(lambda own, number: routed_block(jax.random.fold_in(key_of[1], 2), own, number, TOK_DEV, EXPERTS, 2, CAP, 2))(expert_ids_keys, expert_ids_turns).reshape((TOKENS, 2))
    gate_weights = jnp.clip(0.2 + 0.8 * jax.random.uniform(key_of[2], (TOKENS, 2), jnp.float32) ** shard_levels(key_of[2], (TOKENS, 2), ((0, 256),), -0.2, 0.2), 0.2, 1.0)
    cotangent = heavy_noise(key_of[3], (TOKENS, D), 1.0, 24.0, ((0, 256),), (0, 1, 256, 6.0))
    w_in = noise(key_of[4], (EXPERTS, D, HID), D ** -0.5, 0.1875, ((0, 8),))
    w_out = noise(key_of[5], (EXPERTS, HID, D), HID ** -0.5, 0.125, ((0, 8),))
    return dict(frames=frames, expert_ids=expert_ids, gate_weights=gate_weights, cotangent=cotangent, w_in=w_in, w_out=w_out)


def normalize(values):
    center = values - lax.optimization_barrier(jnp.mean(values, axis=-1, keepdims=True))
    inverse = lax.rsqrt(lax.optimization_barrier(jnp.mean(center * center, axis=-1, keepdims=True)) + 1e-05)
    return (center * inverse, inverse)

def slot_index(id_block):
    flat_ids = id_block.reshape(-1).astype(jnp.int32)
    one_hot = (flat_ids[:, None] == jnp.arange(EXPERTS, dtype=jnp.int32)[None, :]).astype(jnp.int32)
    earlier = jnp.cumsum(one_hot, axis=0) - one_hot
    return (flat_ids * CAP + lax.optimization_barrier(jnp.sum(earlier * one_hot, axis=1))).astype(jnp.int32)

def place(rows, target):
    return jnp.zeros((EXPERTS * CAP, D), jnp.bfloat16).at[target].set(rows)

def to_experts(sent):
    return sent.reshape(N_EXPERT, EXPERTS, CAP, D).transpose(1, 0, 2, 3)

def to_sources(done):
    return done.transpose(1, 0, 2, 3).reshape(N_EXPERT, EXPERTS * CAP, D)

def rounded_term(term):
    narrow = lax.optimization_barrier(term.astype(jnp.bfloat16))
    return narrow.astype(jnp.float32)

def reference(frames, expert_ids, gate_weights, cotangent, w_in, w_out):
    w_in32 = w_in.astype(jnp.float32)
    w_out32 = w_out.astype(jnp.float32)

    def group_step(carry, inputs):
        frame_grp, ids_grp, gate_grp, cot_grp = inputs
        values = frame_grp.astype(jnp.float32)
        standardized, inverse = normalize(values)
        normed = standardized.astype(jnp.bfloat16)
        target = jax.vmap(slot_index)(ids_grp)
        received = to_experts(jax.vmap(place)(jnp.repeat(normed, 2, axis=1), target))
        pre_act = jnp.einsum('escd,edh->esch', received.astype(jnp.float32), w_in32)
        sigma = jax.nn.sigmoid(pre_act)
        hidden = (pre_act * sigma).astype(jnp.bfloat16)
        expert_out = jnp.einsum('esch,ehd->escd', hidden.astype(jnp.float32), w_out32).astype(jnp.bfloat16)
        returned = to_sources(expert_out)
        picked = jax.vmap(lambda block_rows, where: jnp.take(block_rows, where, axis=0))(returned, target)
        flat_gates = gate_grp.astype(jnp.float32).reshape(N_EXPERT, 2 * TOK_DEV, 1)
        weighted = (picked.astype(jnp.float32) * flat_gates).reshape(N_EXPERT, TOK_DEV, 2, D).sum(axis=2)
        mixed = (values + 0.5 * weighted).astype(jnp.bfloat16)
        upstream = cot_grp.astype(jnp.float32)
        grad_rows = (jnp.repeat(upstream, 2, axis=1) * (0.5 * flat_gates)).astype(jnp.bfloat16)
        grad_recv = to_experts(jax.vmap(place)(grad_rows, target))
        term_out = jnp.einsum('esch,escd->ehd', hidden.astype(jnp.float32), grad_recv.astype(jnp.float32))
        grad_hidden = jnp.einsum('escd,ehd->esch', grad_recv.astype(jnp.float32), w_out32)
        grad_pre = (grad_hidden * (sigma + pre_act * sigma * (1.0 - sigma))).astype(jnp.bfloat16)
        term_in = jnp.einsum('escd,esch->edh', received.astype(jnp.float32), grad_pre.astype(jnp.float32))
        grad_back = jnp.einsum('esch,edh->escd', grad_pre.astype(jnp.float32), w_in32).astype(jnp.bfloat16)
        back_rows = to_sources(grad_back)
        picked_back = jax.vmap(lambda block_rows, where: jnp.take(block_rows, where, axis=0))(back_rows, target)
        grad_normed = picked_back.astype(jnp.float32).reshape(N_EXPERT, TOK_DEV, 2, D).sum(axis=2)
        centered = grad_normed - lax.optimization_barrier(jnp.mean(grad_normed, axis=-1, keepdims=True))
        along = standardized * lax.optimization_barrier(jnp.mean(grad_normed * standardized, axis=-1, keepdims=True))
        grad_frames = (upstream + inverse * (centered - along)).astype(jnp.bfloat16)
        return ((carry[0] + rounded_term(term_in), carry[1] + rounded_term(term_out)), (mixed, grad_frames))
    inputs = (frames.reshape(N_DP, N_EXPERT, TOK_DEV, D), expert_ids.reshape(N_DP, N_EXPERT, TOK_DEV, 2), gate_weights.reshape(N_DP, N_EXPERT, TOK_DEV, 2), cotangent.reshape(N_DP, N_EXPERT, TOK_DEV, D))
    start = (jnp.zeros((EXPERTS, D, HID), jnp.float32), jnp.zeros((EXPERTS, HID, D), jnp.float32))
    sums, outputs = lax.scan(group_step, start, inputs)
    mixed = outputs[0].reshape(TOKENS, D)
    grad_frames = outputs[1].reshape(TOKENS, D)
    return (mixed, grad_frames, sums[0], sums[1])
```

```python
import functools

import jax
import jax.numpy as jnp
import numpy as np
from jax import lax
from jax.experimental import pallas as pl
from jax.experimental.pallas import tpu as pltpu
from jax.sharding import Mesh
from jax.sharding import PartitionSpec as P

INTERPRET = False

BF = jnp.bfloat16
F32 = jnp.float32
ALL = ("z", "y", "x", "c")
CAP = 64
SRC = 8
BLK = 256


def call(body, out_shape, grid, in_specs, out_specs, flops, bytes_, scratch=(), prefetch=1):
    return pl.pallas_call(
        body,
        out_shape=out_shape,
        grid_spec=pltpu.PrefetchScalarGridSpec(
            num_scalar_prefetch=prefetch,
            grid=grid,
            in_specs=in_specs,
            out_specs=out_specs,
            scratch_shapes=scratch,
        ),
        cost_estimate=pl.CostEstimate(flops=flops, bytes_accessed=bytes_, transcendentals=0),
        interpret=INTERPRET,
    )


def whole(shape):
    return pl.BlockSpec(shape, lambda i, sc: (0,) * len(shape))


def hop(axis, step):
    def go(value):
        n = lax.axis_size(axis)
        pairs = [
            (2 * i + c, 2 * ((i + (1 - 2 * c) * step) % n) + c) for i in range(n) for c in range(2)
        ]
        return lax.ppermute(value, (axis, "c"), pairs)

    return go


def swap(value):
    return lax.ppermute(value, "c", [(0, 1), (1, 0)])


def spread(own):
    a = hop("x", 1)(own)
    b = hop("x", -1)(own)
    o2 = swap(own)
    t = hop("x", 1)(a)
    return [own, o2, a, b, swap(a), swap(b), t, swap(t)]


PIECES = [(0, 0), (0, 1), (-1, 0), (1, 0), (1, 1), (-1, 1), (2, 0), (2, 1)]


def ring_sum(terms, axis):
    n = len(terms)
    fwd, bwd = hop(axis, 1), hop(axis, -1)
    a = b = None
    for k in range(n // 2, 0, -1):
        a = fwd(terms[k] if a is None else a + terms[k])
        j = n - k + 1
        if k > 1:
            b = bwd(terms[j] if b is None else b + terms[j])
    out = terms[0].astype(F32) + a.astype(F32)
    return out if b is None else out + b.astype(F32)


def emit_order(n):
    order = []
    for k in range(n // 2, 0, -1):
        order.append(k)
        if k > 1:
            order.append(n - k + 1)
    return order + [0]


def one_hots(meta, expert):
    tok = meta.shape[-1]
    hit0 = (meta[:, 0, :] == expert).astype(F32)
    hit1 = (meta[:, 1, :] == expert).astype(F32)
    hit = hit0 + hit1
    gate = hit0 * meta[:, 2, :] + hit1 * meta[:, 3, :]
    row = lax.broadcasted_iota(jnp.int32, (tok, tok), 0)
    col = lax.broadcasted_iota(jnp.int32, (tok, tok), 1)
    earlier = (row < col).astype(BF)
    place = jnp.dot(hit.astype(BF), earlier, preferred_element_type=F32).astype(jnp.int32)
    place = jnp.where(hit > 0, place, -1)
    return place, gate


def pick(place, s, tok):
    slot = lax.broadcasted_iota(jnp.int32, (CAP, tok), 0)
    return slot == place[s : s + 1, :]


def gathered_meta(meta_ref, sc):
    return jnp.concatenate([meta_ref[sc[p]][None] for p in range(SRC)], axis=0)


def fwd_body(sc, meta_ref, *refs):
    pieces, (w_ref, x_ref, hid_ref, slope_ref) = refs[:SRC], refs[SRC:]
    rows, width = SRC * CAP, x_ref.shape[-1]

    @pl.when(pl.program_id(0) == 0)
    def _():
        place, _ = one_hots(gathered_meta(meta_ref, sc), sc[8].astype(F32))
        for p in range(SRC):
            tok = pieces[p].shape[0]
            hot = pick(place, p, tok).astype(BF)
            v = jnp.dot(hot, pieces[p][...], preferred_element_type=F32)
            center = v - jnp.mean(v, axis=-1, keepdims=True)
            inverse = lax.rsqrt(jnp.mean(center * center, axis=-1, keepdims=True) + 1e-05)
            x_ref[sc[p]] = (center * inverse).astype(BF)

    pre = jnp.dot(x_ref[...].reshape(rows, width), w_ref[...], preferred_element_type=F32)
    sigma = jax.nn.sigmoid(pre)
    hid_ref[...] = (pre * sigma).astype(BF)
    slope_ref[...] = sigma + pre * sigma * (1.0 - sigma)


def forward(sc, meta, pieces, w_in):
    tok, width = pieces[0].shape
    hid = w_in.shape[2]
    rows = SRC * CAP
    return call(
        fwd_body,
        (
            jax.ShapeDtypeStruct((SRC, CAP, width), BF),
            jax.ShapeDtypeStruct((rows, hid), BF),
            jax.ShapeDtypeStruct((rows, hid), F32),
        ),
        (hid // BLK,),
        [whole(meta.shape)]
        + [whole((tok, width))] * SRC
        + [pl.BlockSpec((None, width, BLK), lambda i, sc: (0, 0, i))],
        [
            whole((SRC, CAP, width)),
            pl.BlockSpec((rows, BLK), lambda i, sc: (0, i)),
            pl.BlockSpec((rows, BLK), lambda i, sc: (0, i)),
        ],
        2 * rows * width * hid,
        12 << 20,
    )(sc, meta, *pieces, w_in)


def out_body(sc, hid_ref, w_ref, o_ref, acc):
    i = pl.program_id(0)
    part = jnp.dot(hid_ref[...], w_ref[...], preferred_element_type=F32)

    @pl.when(i == 0)
    def _():
        acc[...] = part

    @pl.when(i > 0)
    def _():
        acc[...] += part

    @pl.when(i == pl.num_programs(0) - 1)
    def _():
        o_ref[...] = acc[...].astype(BF)


def expert_out(sc, hidden, w_out):
    rows, hid = hidden.shape
    width = w_out.shape[2]
    blk = 512
    return call(
        out_body,
        jax.ShapeDtypeStruct((rows, width), BF),
        (hid // blk,),
        [
            pl.BlockSpec((rows, blk), lambda i, sc: (0, i)),
            pl.BlockSpec((None, blk, width), lambda i, sc: (0, i, 0)),
        ],
        whole((rows, width)),
        2 * rows * width * hid,
        7 << 20,
        scratch=[pltpu.VMEM((rows, width), F32)],
    )(sc, hidden, w_out)


def back_body(sc, gp_ref, w_ref, o_ref, acc):
    i = pl.program_id(0)
    part = lax.dot_general(
        gp_ref[...], w_ref[...], (((1,), (1,)), ((), ())), preferred_element_type=F32
    )

    @pl.when(i == 0)
    def _():
        acc[...] = part

    @pl.when(i > 0)
    def _():
        acc[...] += part

    @pl.when(i == pl.num_programs(0) - 1)
    def _():
        o_ref[...] = acc[...].astype(BF)


def grad_back(sc, gps, w_in):
    rows, half = gps[0].shape
    width = w_in.shape[1]
    blk = half

    def body(sc, g0, g1, w_ref, o_ref, acc):
        i = pl.program_id(0)
        g = jnp.where(i == 0, g0[...], g1[...])
        part = lax.dot_general(
            g, w_ref[...], (((1,), (1,)), ((), ())), preferred_element_type=F32
        )

        @pl.when(i == 0)
        def _():
            acc[...] = part

        @pl.when(i == 1)
        def _():
            o_ref[...] = (acc[...] + part).astype(BF)

    return call(
        body,
        jax.ShapeDtypeStruct((rows, width), BF),
        (2,),
        [
            whole((rows, half)),
            whole((rows, half)),
            pl.BlockSpec((None, width, blk), lambda i, sc: (0, 0, i)),
        ],
        whole((rows, width)),
        4 * rows * width * half,
        7 << 20,
        scratch=[pltpu.VMEM((rows, width), F32)],
    )(sc, *gps, w_in)


def sel_body(sc, meta_ref, *refs):
    pieces, g_ref = refs[:SRC], refs[SRC]
    place, gate = one_hots(gathered_meta(meta_ref, sc), sc[8].astype(F32))
    for p in range(SRC):
        tok = pieces[p].shape[0]
        hot = pick(place, p, tok)
        v = jnp.dot(hot.astype(BF), pieces[p][...], preferred_element_type=F32)
        weight = jnp.sum(jnp.where(hot, gate[p : p + 1, :], 0.0), axis=1, keepdims=True)
        g_ref[sc[p]] = (v * (0.5 * weight)).astype(BF)


def selected(sc, meta, pieces):
    tok, width = pieces[0].shape
    return call(
        sel_body,
        jax.ShapeDtypeStruct((SRC, CAP, width), BF),
        (1,),
        [whole(meta.shape)] + [whole((tok, width))] * SRC,
        whole((SRC, CAP, width)),
        2 * SRC * CAP * tok * width,
        3 << 20,
    )(sc, meta, *pieces)


def wout_body(n_y, sc, hid_ref, g_ref, *outs):
    width = g_ref.shape[-1]
    term = lax.dot_general(
        hid_ref[...],
        g_ref[...].reshape(-1, width),
        (((0,), (0,)), ((), ())),
        preferred_element_type=F32,
    ).astype(BF)
    each, cols = outs[0].shape[-2:]
    for y in range(n_y):
        for h, o in enumerate(outs):
            o[0, sc[17 + y]] = term[y * each : (y + 1) * each, h * cols : (h + 1) * cols]


def grad_out_terms(sc, hidden, g, n_z, n_y, first, count, chunks):
    rows, hid = hidden.shape
    width = g.shape[-1]
    blk = hid // n_z
    each, cols = blk // n_y, width // chunks
    return call(
        functools.partial(wout_body, n_y),
        tuple(jax.ShapeDtypeStruct((count, n_y, each, cols), BF) for _ in range(chunks)),
        (count,),
        [
            pl.BlockSpec((rows, blk), lambda i, sc: (0, sc[9 + first + i])),
            whole(g.shape),
        ],
        [pl.BlockSpec((1, n_y, each, cols), lambda i, sc: (i, 0, 0, 0))] * chunks,
        2 * rows * width * blk * count,
        count << 20,
    )(sc, hidden, g)


def win_body(n_z, n_y, sc, g_ref, x_ref, w_ref, slope_ref, gp_ref, o_ref):
    width = g_ref.shape[-1]
    gh = lax.dot_general(
        g_ref[...].reshape(-1, width),
        w_ref[...],
        (((1,), (1,)), ((), ())),
        preferred_element_type=F32,
    )
    gp = (gh * slope_ref[...]).astype(BF)
    gp_ref[...] = gp
    term = lax.dot_general(
        x_ref[...].reshape(-1, width), gp, (((0,), (0,)), ((), ())), preferred_element_type=F32
    ).astype(BF)
    each = o_ref.shape[2]
    for z in range(n_z):
        for y in range(n_y):
            at = (z * n_y + y) * each
            o_ref[sc[17 + y], sc[21 + z]] = term[at : at + each, :]


def grad_in_terms(sc, g, x, w_out, slope, n_z, n_y, half, halves):
    rows, hid = slope.shape
    width = g.shape[-1]
    cols = hid // halves
    blk = min(BLK, cols)
    steps = cols // blk
    each = width // (n_z * n_y)
    at = half * steps
    return call(
        functools.partial(win_body, n_z, n_y),
        (
            jax.ShapeDtypeStruct((rows, cols), BF),
            jax.ShapeDtypeStruct((n_y, n_z, each, cols), BF),
        ),
        (steps,),
        [
            whole(g.shape),
            whole(x.shape),
            pl.BlockSpec((None, blk, width), lambda i, sc: (0, at + i, 0)),
            pl.BlockSpec((rows, blk), lambda i, sc: (0, at + i)),
        ],
        [
            pl.BlockSpec((rows, blk), lambda i, sc: (0, i)),
            pl.BlockSpec((n_y, n_z, each, blk), lambda i, sc: (0, 0, 0, i)),
        ],
        4 * rows * width * cols,
        10 << 20,
    )(sc, g, x, w_out, slope)


def final_body(sc, ids_ref, gates_ref, f_ref, c_ref, eo_ref, gb_ref, mixed_ref, gf_ref):
    tok = f_ref.shape[0]
    ids = ids_ref[...]
    gates = gates_ref[...]
    lane = lax.broadcasted_iota(jnp.int32, (tok, 128), 1)
    hot0 = lane == ids[:, 0:1]
    hot1 = lane == ids[:, 1:2]
    row = lax.broadcasted_iota(jnp.int32, (tok, tok), 0)
    col = lax.broadcasted_iota(jnp.int32, (tok, tok), 1)
    any_hot = (hot0 | hot1).astype(BF)
    before = jnp.dot((col < row).astype(BF), any_hot, preferred_element_type=F32)
    pos0 = jnp.sum(jnp.where(hot0, before, 0.0), axis=1, keepdims=True).astype(jnp.int32)
    pos1 = jnp.sum(jnp.where(hot1, before, 0.0), axis=1, keepdims=True).astype(jnp.int32)
    slot = lax.broadcasted_iota(jnp.int32, (tok, SRC * CAP), 1)
    s0 = slot == ids[:, 0:1] * CAP + pos0
    s1 = slot == ids[:, 1:2] * CAP + pos1
    eo = eo_ref[...]
    p0 = jnp.dot(s0.astype(BF), eo, preferred_element_type=F32) * gates[:, 0:1]
    p1 = jnp.dot(s1.astype(BF), eo, preferred_element_type=F32) * gates[:, 1:2]
    v = f_ref[...].astype(F32)
    mixed_ref[...] = (v + 0.5 * (p0 + p1)).astype(BF)
    gn = jnp.dot((s0 | s1).astype(BF), gb_ref[...], preferred_element_type=F32)
    center = v - jnp.mean(v, axis=-1, keepdims=True)
    inverse = lax.rsqrt(jnp.mean(center * center, axis=-1, keepdims=True) + 1e-05)
    standardized = center * inverse
    centered = gn - jnp.mean(gn, axis=-1, keepdims=True)
    along = standardized * jnp.mean(gn * standardized, axis=-1, keepdims=True)
    gf_ref[...] = (c_ref[...].astype(F32) + inverse * (centered - along)).astype(BF)


def finish(sc, ids, gates, frames, cotangent, eo, gb):
    tok, width = frames.shape
    return call(
        final_body,
        (jax.ShapeDtypeStruct((tok, width), BF),) * 2,
        (1,),
        [whole(a.shape) for a in (ids, gates, frames, cotangent, eo, gb)],
        [whole((tok, width))] * 2,
        6 * SRC * CAP * tok * width,
        3 << 20,
    )(sc, ids, gates, frames, cotangent, eo, gb)


def tables(n_z, n_y):
    z, y, x, c = (lax.axis_index(a) for a in ALL)
    sign = 1 - 2 * c
    k = np.array([dx for dx, _ in PIECES] + [0], np.int32)
    flip = np.array([f for _, f in PIECES] + [0], np.int32)
    src = 2 * ((x + sign * k + 4) % 4) + (c + flip) % 2
    order = np.array(emit_order(n_z) + [0] * (8 - n_z), np.int32)
    blocks = (z + sign * order + 2 * n_z) % n_z
    ys = (sign * (np.arange(4, dtype=np.int32) - y) + 4 * n_y) % n_y
    zs = (sign * (np.arange(8, dtype=np.int32) - z) + 8 * n_z) % n_z
    return jnp.concatenate([src, blocks, ys, zs]).astype(jnp.int32)


def routed_back(rows):
    width = rows.shape[-1]
    sent = rows.reshape(SRC, CAP, width)
    return lax.all_to_all(sent, ("x", "c"), split_axis=0, concat_axis=0, tiled=True).reshape(
        SRC * CAP, width
    )


def per_device(frames, expert_ids, gate_weights, cotangent, w_in, w_out):
    n_z, n_y = lax.axis_size("z"), lax.axis_size("y")
    tok = frames.shape[0]
    sc = tables(n_z, n_y)
    own_meta = jnp.concatenate([expert_ids.T.astype(F32), gate_weights.T], axis=0)
    meta = lax.all_to_all(
        jnp.broadcast_to(own_meta[None], (SRC, 4, tok)), ("x", "c"), split_axis=0, concat_axis=0, tiled=True
    )
    f_pieces = spread(frames)
    c_pieces = spread(cotangent)
    x, hidden, slope = forward(sc, meta, f_pieces, w_in)
    eo = expert_out(sc, hidden, w_out)
    g = selected(sc, meta, c_pieces)

    chunks = 2
    order = emit_order(n_z)
    parts = [
        grad_out_terms(sc, hidden, g, n_z, n_y, 0, 2, chunks),
        grad_out_terms(sc, hidden, g, n_z, n_y, 2, n_z - 2, chunks),
    ]
    grad_out = []
    for h in range(chunks):
        terms = [None] * n_z
        for i, j in enumerate(order):
            terms[j] = parts[0][h][i] if i < 2 else parts[1][h][i - 2]
        total = ring_sum(terms, "z")
        low = total.astype(BF)
        grad_out.append(ring_sum([low[j] for j in range(n_y)], "y"))
    gps, grad_in = [], []
    for h in range(2):
        gp, win = grad_in_terms(sc, g, x, w_out, slope, n_z, n_y, h, 2)
        gps.append(gp)
        total = ring_sum([win[j] for j in range(n_y)], "y")
        low = total.astype(BF)
        grad_in.append(ring_sum([low[j] for j in range(n_z)], "z"))
    gb = grad_back(sc, gps, w_in)
    eo_back = routed_back(eo)
    gb_back = routed_back(gb)
    mixed, grad_frames = finish(sc, expert_ids, gate_weights, frames, cotangent, eo_back, gb_back)
    return (
        mixed,
        grad_frames,
        jnp.concatenate(grad_in, axis=1)[None],
        jnp.concatenate(grad_out, axis=1)[None],
    )


def solution(mesh):
    n = mesh.shape["dp"]
    shape = (8, 4, 4, 2) if n == 32 else (n // 2, 2, 4, 2)
    finer = Mesh(mesh.devices.reshape(shape), ALL)
    rows = P(ALL, None)
    weight = P(("x", "c"), None, None)
    grads = P(("x", "c"), ("z", "y"), None)
    return jax.shard_map(
        per_device,
        mesh=finer,
        in_specs=(rows, rows, rows, rows, weight, weight),
        out_specs=(rows, rows, grads, grads),
        check_vma=False,
    )
```

```python
import functools

import jax
import jax.numpy as jnp
import numpy as np
from jax import lax
from jax.experimental import pallas as pl
from jax.experimental.pallas import tpu as pltpu
from jax.sharding import Mesh
from jax.sharding import PartitionSpec as P

INTERPRET = False

BF = jnp.bfloat16
F32 = jnp.float32
ALL = ("z", "y", "x", "c")
CAP = 64
SRC = 8


def call(body, out_shape, grid, in_specs, out_specs, flops, bytes_, mib):
    return pl.pallas_call(
        body,
        out_shape=out_shape,
        grid_spec=pltpu.PrefetchScalarGridSpec(
            num_scalar_prefetch=1, grid=grid, in_specs=in_specs, out_specs=out_specs
        ),
        cost_estimate=pl.CostEstimate(flops=flops, bytes_accessed=bytes_, transcendentals=0),
        compiler_params=pltpu.CompilerParams(vmem_limit_bytes=mib << 20),
        interpret=INTERPRET,
    )


def mm(a, b, dims=((1,), (0,))):
    if INTERPRET:
        a, b = a.astype(F32), b.astype(F32)
    return lax.dot_general(a, b, (dims, ((), ())), preferred_element_type=F32)


def whole(shape):
    return pl.BlockSpec(shape, lambda i, sc: (0,) * len(shape))


def hop(axis, step):
    def go(value):
        n = lax.axis_size(axis)
        pairs = [
            (2 * i + c, 2 * ((i + (1 - 2 * c) * step) % n) + c) for i in range(n) for c in range(2)
        ]
        return lax.ppermute(value, (axis, "c"), pairs)

    return go


def swap(value):
    return lax.ppermute(value, "c", [(0, 1), (1, 0)])


def spread(own):
    a = hop("x", 1)(own)
    b = hop("x", -1)(own)
    o2 = swap(own)
    t = hop("x", 1)(a)
    return [own, o2, a, b, swap(a), swap(b), t, swap(t)]


PIECES = [(0, 0), (0, 1), (-1, 0), (1, 0), (1, 1), (-1, 1), (2, 0), (2, 1)]


def ring_sum(terms, axis):
    n = len(terms)
    fwd, bwd = hop(axis, 1), hop(axis, -1)
    a = b = None
    for k in range(n // 2, 0, -1):
        a = fwd(terms[k] if a is None else a + terms[k])
        j = n - k + 1
        if k > 1:
            b = bwd(terms[j] if b is None else b + terms[j])
    out = terms[0].astype(F32) + a.astype(F32)
    return out if b is None else out + b.astype(F32)


def emit_order(n):
    order = []
    for k in range(n // 2, 0, -1):
        order.append(k)
        if k > 1:
            order.append(n - k + 1)
    return order + [0]


def one_hots(sc, meta_ref):
    meta = jnp.concatenate([meta_ref[sc[p]][None] for p in range(SRC)], axis=0)
    tok = meta.shape[-1]
    expert = sc[8].astype(F32)
    hit0 = (meta[:, 0, :] == expert).astype(F32)
    hit1 = (meta[:, 1, :] == expert).astype(F32)
    hit = hit0 + hit1
    gate = hit0 * meta[:, 2, :] + hit1 * meta[:, 3, :]
    row = lax.broadcasted_iota(jnp.int32, (tok, tok), 0)
    col = lax.broadcasted_iota(jnp.int32, (tok, tok), 1)
    earlier = (row < col).astype(BF)
    place = mm(hit.astype(BF), earlier).astype(jnp.int32)
    return jnp.where(hit > 0, place, -1), gate


def pick(place, s, tok):
    slot = lax.broadcasted_iota(jnp.int32, (CAP, tok), 0)
    return slot == place[s : s + 1, :]


def normalize(v):
    center = v - jnp.mean(v, axis=-1, keepdims=True)
    inverse = lax.rsqrt(jnp.mean(center * center, axis=-1, keepdims=True) + 1e-05)
    return center * inverse, inverse


def fwd_body(sc, meta_ref, *refs):
    pieces, (w_ref, x_ref, xt_ref, hid_ref, hidt_ref, slope_ref) = refs[:SRC], refs[SRC:]
    rows, width = SRC * CAP, x_ref.shape[-1]

    @pl.when(pl.program_id(0) == 0)
    def _():
        place, _ = one_hots(sc, meta_ref)
        for p in range(SRC):
            hot = pick(place, p, pieces[p].shape[0]).astype(BF)
            at = pl.multiple_of(sc[p] * CAP, CAP)
            x_ref[pl.ds(at, CAP), :] = mm(hot, pieces[p][...]).astype(BF)

        @pl.loop(0, SRC)
        def _(s):
            at = pl.ds(pl.multiple_of(s * CAP, CAP), CAP)
            x_ref[at, :] = normalize(x_ref[at, :].astype(F32))[0].astype(BF)

        xt_ref[...] = x_ref[...].T

    pre = mm(x_ref[...], w_ref[...])
    sigma = 0.5 + 0.5 * jnp.tanh(0.5 * pre)
    hid = pre * sigma
    low = hid.astype(BF)
    hid_ref[...] = low
    hidt_ref[...] = low.T
    slope_ref[...] = (sigma + hid * (1.0 - sigma)).astype(BF)


def forward(sc, meta, pieces, w_in):
    tok, width = pieces[0].shape
    hid = w_in.shape[2]
    rows = SRC * CAP
    blk = min(512, hid)
    return call(
        fwd_body,
        (
            jax.ShapeDtypeStruct((rows, width), BF),
            jax.ShapeDtypeStruct((width, rows), BF),
            jax.ShapeDtypeStruct((rows, hid), BF),
            jax.ShapeDtypeStruct((hid, rows), BF),
            jax.ShapeDtypeStruct((rows, hid), BF),
        ),
        (hid // blk,),
        [whole(meta.shape)]
        + [whole((tok, width))] * SRC
        + [pl.BlockSpec((None, width, blk), lambda i, sc: (0, 0, i))],
        [
            whole((rows, width)),
            whole((width, rows)),
            pl.BlockSpec((rows, blk), lambda i, sc: (0, i)),
            pl.BlockSpec((blk, rows), lambda i, sc: (i, 0)),
            pl.BlockSpec((rows, blk), lambda i, sc: (0, i)),
        ],
        2 * rows * width * hid,
        14 << 20,
        24,
    )(sc, meta, *pieces, w_in)


def sel_body(sc, meta_ref, *refs):
    pieces, g_ref = refs[:SRC], refs[SRC]
    place, gate = one_hots(sc, meta_ref)
    for p in range(SRC):
        hot = pick(place, p, pieces[p].shape[0])
        v = mm(hot.astype(BF), pieces[p][...])
        weight = jnp.sum(jnp.where(hot, gate[p : p + 1, :], 0.0), axis=1, keepdims=True)
        at = pl.multiple_of(sc[p] * CAP, CAP)
        g_ref[pl.ds(at, CAP), :] = (v * (0.5 * weight)).astype(BF)


def selected(sc, meta, pieces):
    tok, width = pieces[0].shape
    return call(
        sel_body,
        jax.ShapeDtypeStruct((SRC * CAP, width), BF),
        (1,),
        [whole(meta.shape)] + [whole((tok, width))] * SRC,
        whole((SRC * CAP, width)),
        2 * SRC * CAP * tok * width,
        3 << 20,
        12,
    )(sc, meta, *pieces)


def wout_body(n_y, sc, hid_ref, g_ref, out):
    term = mm(hid_ref[...], g_ref[...]).astype(BF)
    each = out.shape[-2]
    for y in range(n_y):
        out[y] = term[y * each : (y + 1) * each, :]


def grad_out_terms(sc, hidden_t, g, n_z, n_y, first, count):
    hid, rows = hidden_t.shape
    width = g.shape[-1]
    blk = hid // n_z
    each = blk // n_y
    return call(
        functools.partial(wout_body, n_y),
        jax.ShapeDtypeStruct((count, n_y, each, width), BF),
        (count,),
        [
            pl.BlockSpec((blk, rows), lambda i, sc: (sc[9 + first + i], 0)),
            whole(g.shape),
        ],
        pl.BlockSpec((None, n_y, each, width), lambda i, sc: (i, 0, 0, 0)),
        2 * rows * width * blk * count,
        count << 20,
        12,
    )(sc, hidden_t, g)


def win_body(n_z, n_y, sc, g_ref, xt_ref, w_ref, slope_ref, gp_ref, o_ref):
    gh = mm(g_ref[...], w_ref[...], ((1,), (1,)))
    gp = (gh * slope_ref[...].astype(F32)).astype(BF)
    gp_ref[...] = gp
    each = o_ref.shape[2]
    term = mm(xt_ref[...], gp).astype(BF)
    for z in range(n_z):
        for y in range(n_y):
            at = (z * n_y + y) * each
            o_ref[sc[17 + y], sc[21 + z]] = term[at : at + each, :]


def grad_in_terms(sc, g, xt, w_out, slope, n_z, n_y):
    rows, hid = slope.shape
    width = g.shape[-1]
    blk = min(512, hid)
    each = width // (n_z * n_y)
    return call(
        functools.partial(win_body, n_z, n_y),
        (
            jax.ShapeDtypeStruct((rows, hid), BF),
            jax.ShapeDtypeStruct((n_y, n_z, each, hid), BF),
        ),
        (hid // blk,),
        [
            whole(g.shape),
            whole(xt.shape),
            pl.BlockSpec((None, blk, width), lambda i, sc: (0, i, 0)),
            pl.BlockSpec((rows, blk), lambda i, sc: (0, i)),
        ],
        [
            pl.BlockSpec((rows, blk), lambda i, sc: (0, i)),
            pl.BlockSpec((n_y, n_z, each, blk), lambda i, sc: (0, 0, 0, i)),
        ],
        4 * rows * width * hid,
        14 << 20,
        24,
    )(sc, g, xt, w_out, slope)


def final_body(sc, meta_ref, f_ref, c_ref, eo_ref, gb_ref, mixed_ref, gf_ref):
    tok = f_ref.shape[0]
    meta = meta_ref[...].T
    ids = meta[:, 0:2].astype(jnp.int32)
    lane = lax.broadcasted_iota(jnp.int32, (tok, 128), 1)
    hot0 = lane == ids[:, 0:1]
    hot1 = lane == ids[:, 1:2]
    row = lax.broadcasted_iota(jnp.int32, (tok, tok), 0)
    col = lax.broadcasted_iota(jnp.int32, (tok, tok), 1)
    any_hot = (hot0 | hot1).astype(BF)
    before = mm((col < row).astype(BF), any_hot)
    pos0 = jnp.sum(jnp.where(hot0, before, 0.0), axis=1, keepdims=True).astype(jnp.int32)
    pos1 = jnp.sum(jnp.where(hot1, before, 0.0), axis=1, keepdims=True).astype(jnp.int32)
    slot = lax.broadcasted_iota(jnp.int32, (tok, SRC * CAP), 1)
    s0 = slot == ids[:, 0:1] * CAP + pos0
    s1 = slot == ids[:, 1:2] * CAP + pos1
    eo = eo_ref[...]
    p0 = mm(s0.astype(BF), eo) * meta[:, 2:3]
    p1 = mm(s1.astype(BF), eo) * meta[:, 3:4]
    v = f_ref[...].astype(F32)
    mixed_ref[...] = (v + 0.5 * (p0 + p1)).astype(BF)
    gn = mm((s0 | s1).astype(BF), gb_ref[...])
    standardized, inverse = normalize(v)
    centered = gn - jnp.mean(gn, axis=-1, keepdims=True)
    along = standardized * jnp.mean(gn * standardized, axis=-1, keepdims=True)
    gf_ref[...] = (c_ref[...].astype(F32) + inverse * (centered - along)).astype(BF)


def finish(sc, meta, frames, cotangent, eo, gb):
    tok, width = frames.shape
    return call(
        final_body,
        (jax.ShapeDtypeStruct((tok, width), BF),) * 2,
        (1,),
        [whole(a.shape) for a in (meta, frames, cotangent, eo, gb)],
        [whole((tok, width))] * 2,
        6 * SRC * CAP * tok * width,
        4 << 20,
        16,
    )(sc, meta, frames, cotangent, eo, gb)


def tables(n_z, n_y):
    z, y, x, c = (v.reshape(-1, 1) for v in np.indices((n_z, n_y, 4, 2)))
    sign = 1 - 2 * c
    k = np.array([dx for dx, _ in PIECES] + [0])
    flip = np.array([f for _, f in PIECES] + [0])
    src = 2 * ((x + sign * k) % 4) + (c + flip) % 2
    order = np.array(emit_order(n_z) + [0] * (8 - n_z))
    blocks = (z + sign * order) % n_z
    ys = (sign * (np.arange(4) - y)) % n_y
    zs = (sign * (np.arange(8) - z)) % n_z
    return np.concatenate([src, blocks, ys, zs], axis=1).astype(np.int32)


def routed_back(rows):
    width = rows.shape[-1]
    sent = rows.reshape(SRC, CAP, width)
    return lax.all_to_all(sent, ("x", "c"), split_axis=0, concat_axis=0, tiled=True).reshape(
        SRC * CAP, width
    )


def per_device(frames, expert_ids, gate_weights, cotangent, w_in, w_out):
    n_z, n_y = lax.axis_size("z"), lax.axis_size("y")
    tok, width = frames.shape
    hid = w_in.shape[2]
    sc = jnp.asarray(tables(n_z, n_y))[lax.axis_index(ALL)]
    ids = expert_ids.T.astype(F32)
    own_meta = jnp.concatenate([ids, gate_weights.T, ids, gate_weights.T], axis=0)
    meta = lax.all_to_all(
        jnp.broadcast_to(own_meta[None], (SRC, 8, tok)), ("x", "c"), split_axis=0, concat_axis=0, tiled=True
    )
    f_pieces = spread(frames)
    c_pieces = spread(cotangent)
    x, xt, hidden, hidden_t, slope = forward(sc, meta, f_pieces, w_in)
    eo = mm(hidden, w_out[0]).astype(BF)
    g = selected(sc, meta, c_pieces)

    order = emit_order(n_z)
    parts = [
        grad_out_terms(sc, hidden_t, g, n_z, n_y, 0, 2),
        grad_out_terms(sc, hidden_t, g, n_z, n_y, 2, n_z - 2),
    ]
    terms = [None] * n_z
    for i, j in enumerate(order):
        terms[j] = parts[0][i] if i < 2 else parts[1][i - 2]
    low = ring_sum(terms, "z").astype(BF)
    arrived = lax.all_to_all(low, "y", split_axis=0, concat_axis=0, tiled=True)
    grad_out = jnp.sum(arrived.astype(F32), axis=0)

    gp, win = grad_in_terms(sc, g, xt, w_out, slope, n_z, n_y)
    low = ring_sum([win[j] for j in range(n_y)], "y").astype(BF)
    grad_in = ring_sum([low[j] for j in range(n_z)], "z")
    gb = mm(gp, w_in[0], ((1,), (1,))).astype(BF)
    eo_back = routed_back(eo)
    gb_back = routed_back(gb)
    mixed, grad_frames = finish(sc, own_meta, frames, cotangent, eo_back, gb_back)
    return mixed, grad_frames, grad_in[None], grad_out[None]


def solution(mesh):
    n = mesh.shape["dp"]
    shape = (8, 4, 4, 2) if n == 32 else (n // 2, 2, 4, 2)
    finer = Mesh(mesh.devices.reshape(shape), ALL)
    rows = P(ALL, None)
    weight = P(("x", "c"), None, None)
    grads = P(("x", "c"), ("z", "y"), None)
    return jax.shard_map(
        per_device,
        mesh=finer,
        in_specs=(rows, rows, rows, rows, weight, weight),
        out_specs=(rows, rows, grads, grads),
        check_vma=False,
    )
```
